512 devices in a mesh: replica: 32 (over x, z), tensor: 16 (over y, core).
Axes of the slice: x: 4, y: 8, z: 8, core: 2. Of those that a mesh axis runs over, the one named last changes fastest.
Arguments:
- tokens: bfloat16 [1536, 1536], P(('replica', 'tensor')), may hold values from -6 to 6
- attn_gain: float32 [1536], replicated, may hold values from 0.5 to 1.5
- qkv_weight: bfloat16 [1536, 2560], P(None, 'tensor'), may hold values from -0.15625 to 0.15625
- out_weight: bfloat16 [1536, 1536], P('tensor'), may hold values from -0.15625 to 0.15625
- moe_gain: float32 [1536], replicated, may hold values from 0.5 to 1.5
- router: bfloat16 [1536, 8], replicated, may hold values from -0.15625 to 0.15625
- expert_gate_up: bfloat16 [1536, 2, 4096], P(None, None, 'tensor'), may hold values from -0.15625 to 0.15625
- expert_down: bfloat16 [4096, 1536], P('tensor'), may hold values from -0.25 to 0.25
- kv_cache: bfloat16 [3072, 2, 128, 512], P(('replica', 'tensor')), may hold values from -240 to 240
- page_table: int32 [1024, 2], P('replica'), may hold values from 0 to 93, as said below
- home_len: int32 [1024], P('replica'), may hold values from 1 to 256
- guest_source: int32 [512], P(('replica', 'tensor')), may hold values from 0 to 31, as said below
- guest_pages: int32 [512, 2], P(('replica', 'tensor')), may hold values from 4 to 5, as said below
- guest_len: int32 [512], P(('replica', 'tensor')), may hold values from 1 to 256
- routes: int32 [1536, 6], P('replica'), may hold values from 0 to 7, all different within a row
Outputs:
- layer_out: bfloat16 [1536, 1536], P(('replica', 'tensor'))
The draws below stay inside these ranges and needn't reach their ends.
Inputs may be any that keep to these rules, and one draw needn't show every extreme that they name: `page_table`: the home requests of one replica name different pages, together each of a device's first 4 pages exactly once. `guest_source`: never the guest's own replica; among the guests of one slot and one tensor index, each replica is named exactly once. `guest_pages`: each row names 2 different pages, none of them named by a home request, and guests of different slots name different pages.
All inputs are finite; a program needn't handle non-finite values.
Results may differ from the reference program's by a relative error of at most 0.022.
Values may be sent and summed in bfloat16 or wider, within the bound.
A program may use at most 64 MiB of HBM per device.

```python
import jax
import jax.numpy as jnp
from jax import lax

D = 1536
HEADS = 12
KVH = 4
HD = 128
MOE_FF = 512
TOP = 6
EXPERTS = 8
PAGE = 128
MAXP = 2
HOME_DEV = 2
GUEST_DEV = 1
PAGES_DEV = 6
ROWS_DEV = 3
TOKENS_REP = 48
ROWS = 1536
HOMES_REP = 32
POOL = 96
REPLICAS = 32
GUESTS = 512
GROUP = 3
QKV = 2560
UNITS = 4096


def draw_kv_cache(key, part):
    shape = (REPLICAS * POOL, 2, PAGE, KVH * HD)
    base = jnp.clip(jax.random.normal(key, shape, jnp.float32), -6.0, 6.0)
    return base.astype(jnp.bfloat16)


def draw_page_table(key, part):
    per_device = HOME_DEV * MAXP
    replica_keys = jax.random.split(key, REPLICAS)
    items = jax.vmap(lambda single: jax.random.permutation(single, HOMES_REP * MAXP))(replica_keys)
    pages = items // per_device * PAGES_DEV + items % per_device
    return pages.reshape(REPLICAS * HOMES_REP, MAXP).astype(jnp.int32)


def draw_guest_source(key, part):
    lanes = GUESTS // REPLICAS
    lane_keys = jax.random.split(key, lanes)
    orders = jax.vmap(lambda single: jax.random.permutation(single, REPLICAS))(lane_keys).astype(jnp.int32)
    places = jnp.argsort(orders, axis=1).astype(jnp.int32)
    following = jnp.take_along_axis(orders, (places + 1) % REPLICAS, axis=1)
    return following.T.reshape(GUESTS).astype(jnp.int32)


def draw_guest_pages(key, part):
    row_keys = jax.random.split(key, GUESTS)
    orders = jax.vmap(lambda single: jax.random.permutation(single, MAXP))(row_keys).astype(jnp.int32)
    slot = jnp.arange(GUESTS, dtype=jnp.int32) % GUEST_DEV
    return (HOME_DEV * MAXP + slot[:, None] * MAXP + orders).astype(jnp.int32)


def set_ends(array, rng, least, top_value):
    extent = array.shape
    place = [jax.random.randint(jax.random.fold_in(rng, axis), (), 0, extent[axis]) for axis in range(len(extent))]
    array = array.at[tuple(place)].set(least)
    longest = extent.index(max(extent))
    place[longest] = (place[longest] + 1) % extent[longest]
    return array.at[tuple(place)].set(top_value)


def block_levels(rng, extent, shards, least, top_value):
    def one(axis_at, blocks):
        draws = jax.random.uniform(jax.random.fold_in(jax.random.fold_in(rng, 6), axis_at), (blocks,), jnp.float32, least / len(shards), top_value / len(shards))
        return jnp.repeat(jnp.exp(draws), extent[axis_at] // blocks).reshape((-1,) + (1,) * (len(extent) - axis_at - 1))

    level = one(*shards[0])
    for cut in shards[1:]:
        level = level * one(*cut)
    return level


def choose_distinct(key, rows, count, top, lift):
    ranking = jax.random.permutation(jax.random.fold_in(key, 1), count)
    favour = ranking
    for power in range(3):
        favour = favour * favour // count
    favour = favour * lift // count
    chance = jax.random.randint(jax.random.fold_in(key, 2), (rows, count), 0, 4096) + favour
    sure = jax.random.permutation(jax.random.fold_in(key, 3), rows)[jnp.arange(count) % rows]
    chance = jnp.where(jnp.arange(rows)[:, None] == sure[None, :], 1 << 14, chance)
    priority = chance * count + jnp.arange(count)
    return lax.top_k(priority.astype(jnp.int32), top)[1].astype(jnp.int32)


def bell_draw(stream_key, dims, spread, bound, shards=(), kind=jnp.bfloat16):
    result = spread * jax.random.normal(stream_key, dims, jnp.float32)
    if shards:
        result = result * block_levels(stream_key, dims, shards, -0.22, 0.18)
    return jnp.clip(result, -bound, bound).astype(kind)


def setup_inputs(seed: int = 0) -> dict:
    streams_of = jax.random.split(jax.random.key(seed), 16)
    tokens = bell_draw(streams_of[0], (ROWS, D), 1.0, 6.0, ((0, 512),))
    attn_gain = jnp.clip(1.0 + 0.1 * jax.random.normal(streams_of[1], (D,), jnp.float32), 0.5, 1.5)
    qkv_weight = bell_draw(streams_of[2], (D, QKV), D ** -0.5, 0.15625, ((1, 16),))
    out_weight = bell_draw(streams_of[3], (HEADS * HD, D), (HEADS * HD) ** -0.5, 0.15625, ((0, 16),))
    moe_gain = jnp.clip(1.0 + 0.1 * jax.random.normal(streams_of[4], (D,), jnp.float32), 0.5, 1.5)
    router = bell_draw(streams_of[5], (D, EXPERTS), D ** -0.5, 0.15625)
    expert_gate_up = bell_draw(streams_of[6], (D, 2, UNITS), D ** -0.5, 0.15625, ((2, 16),))
    expert_down = bell_draw(streams_of[7], (UNITS, D), MOE_FF ** -0.5, 0.25, ((0, 16),))
    kv_cache = draw_kv_cache(jax.random.fold_in(streams_of[15], 71), 0)
    page_table = draw_page_table(jax.random.fold_in(streams_of[15], 71), 0)
    home_len = set_ends(jax.random.randint(streams_of[10], (REPLICAS * HOMES_REP,), 1, MAXP * PAGE + 1), jax.random.fold_in(streams_of[10], 1), 1, MAXP * PAGE).astype(jnp.int32)
    guest_source = draw_guest_source(jax.random.fold_in(streams_of[15], 71), 0)
    guest_pages = draw_guest_pages(jax.random.fold_in(streams_of[15], 71), 0)
    guest_len = set_ends(jax.random.randint(streams_of[13], (GUESTS,), 1, MAXP * PAGE + 1), jax.random.fold_in(streams_of[13], 1), 1, MAXP * PAGE).astype(jnp.int32)
    routes = choose_distinct(streams_of[14], ROWS, EXPERTS, TOP, 6144)
    return dict(tokens=tokens, attn_gain=attn_gain, qkv_weight=qkv_weight, out_weight=out_weight, moe_gain=moe_gain, router=router, expert_gate_up=expert_gate_up, expert_down=expert_down, kv_cache=kv_cache, page_table=page_table, home_len=home_len, guest_source=guest_source, guest_pages=guest_pages, guest_len=guest_len, routes=routes)


def normed_rows(values, gain):
    widened = values.astype(jnp.float32)
    inverse = lax.rsqrt(lax.optimization_barrier(jnp.mean(widened * widened, axis=-1, keepdims=True)) + 1e-05)
    return (widened * inverse * gain).astype(jnp.bfloat16)

def reference(tokens, attn_gain, qkv_weight, out_weight, moe_gain, router, expert_gate_up, expert_down, kv_cache, page_table, home_len, guest_source, guest_pages, guest_len, routes):
    projected = jnp.dot(normed_rows(tokens, attn_gain), qkv_weight, preferred_element_type=jnp.float32).astype(jnp.bfloat16)
    row_ids = jnp.arange(ROWS, dtype=jnp.int32)
    replica_of = row_ids // TOKENS_REP
    column_of = row_ids % TOKENS_REP // ROWS_DEV
    slot_of = row_ids % ROWS_DEV
    is_home = slot_of < HOME_DEV
    home_index = replica_of * HOMES_REP + column_of * HOME_DEV + jnp.minimum(slot_of, HOME_DEV - 1)
    guest_index = row_ids // ROWS_DEV * GUEST_DEV + jnp.maximum(slot_of - HOME_DEV, 0)
    home_ids = replica_of[:, None] * POOL + page_table[home_index]
    guest_ids = guest_source[guest_index][:, None] * POOL + column_of[:, None] * PAGES_DEV + guest_pages[guest_index]
    page_ids = jnp.where(is_home[:, None], home_ids, guest_ids).astype(jnp.int32)
    lengths = jnp.where(is_home, home_len[home_index], guest_len[guest_index]).astype(jnp.int32)
    qwidth = HEADS * HD
    kwidth = KVH * HD
    queries = projected[:, :qwidth].reshape(REPLICAS, TOKENS_REP, KVH, GROUP, HD)
    fresh_keys = projected[:, qwidth:qwidth + kwidth].reshape(REPLICAS, TOKENS_REP, KVH, HD)
    fresh_values = projected[:, qwidth + kwidth:].reshape(REPLICAS, TOKENS_REP, KVH, HD)
    flat_cache = kv_cache.reshape(REPLICAS * POOL, 2, PAGE, KVH, HD)
    positions = jnp.arange(MAXP * PAGE, dtype=jnp.int32)
    scale = HD ** (-0.5)
    highest = lax.Precision.HIGHEST

    def attend(block):
        query, fresh_key, fresh_value, block_ids, block_len = block
        pages = flat_cache[block_ids]
        key_rows = pages[:, :, 0].reshape(TOKENS_REP, MAXP * PAGE, KVH, HD).astype(jnp.float32)
        value_rows = pages[:, :, 1].reshape(TOKENS_REP, MAXP * PAGE, KVH, HD).astype(jnp.float32)
        wide_query = query.astype(jnp.float32)
        scores = jnp.einsum('rkgd,rjkd->rkgj', wide_query, key_rows, precision=highest) * scale
        usable = (positions[None, :] < block_len[:, None])[:, None, None, :]
        scores = jnp.where(usable, scores, -1e+30)
        peak = lax.optimization_barrier(jnp.max(scores, axis=-1))
        weights = jnp.where(usable, jnp.exp(scores - peak[..., None]), 0.0)
        total = lax.optimization_barrier(jnp.sum(weights, axis=-1))
        rounded = lax.optimization_barrier(weights.astype(jnp.bfloat16)).astype(jnp.float32)
        summed = jnp.einsum('rkgj,rjkd->rkgd', rounded, value_rows, precision=highest)
        own_score = jnp.einsum('rkgd,rkd->rkg', wide_query, fresh_key.astype(jnp.float32), precision=highest) * scale
        top = jnp.maximum(peak, own_score)
        factor = jnp.exp(peak - top)
        newest = jnp.exp(own_score - top)
        numerator = summed * factor[..., None] + newest[..., None] * fresh_value.astype(jnp.float32)[:, :, None, :]
        denominator = total * factor + newest
        mixed = numerator / denominator[..., None]
        return mixed.reshape(TOKENS_REP, HEADS * HD).astype(jnp.bfloat16)
    attended = lax.map(attend, (queries, fresh_keys, fresh_values, page_ids.reshape(REPLICAS, TOKENS_REP, MAXP), lengths.reshape(REPLICAS, TOKENS_REP)))
    attended = attended.reshape(ROWS, HEADS * HD)
    hidden = (tokens.astype(jnp.float32) + jnp.dot(attended, out_weight, preferred_element_type=jnp.float32)).astype(jnp.bfloat16)
    normed = normed_rows(hidden, moe_gain)
    logits = jnp.dot(normed, router, preferred_element_type=jnp.float32)
    weights = jax.nn.softmax(jnp.take_along_axis(logits, routes, axis=1), axis=1)
    expert_weight = lax.optimization_barrier(jnp.sum(weights[:, :, None] * (routes[:, :, None] == jnp.arange(EXPERTS, dtype=jnp.int32)[None, None, :]), axis=1))
    per_unit = jnp.repeat(expert_weight, MOE_FF, axis=1)
    gate = jnp.dot(normed, expert_gate_up[:, 0, :], preferred_element_type=jnp.float32)
    upper = jnp.dot(normed, expert_gate_up[:, 1, :], preferred_element_type=jnp.float32)
    activated = (jax.nn.silu(gate) * upper * per_unit).astype(jnp.bfloat16)
    return (hidden.astype(jnp.float32) + jnp.dot(activated, expert_down, preferred_element_type=jnp.float32)).astype(jnp.bfloat16)
```

```python
import functools

import jax
import jax.numpy as jnp
from jax import lax
from jax.experimental import pallas as pl
from jax.experimental.pallas import tpu as pltpu
from jax.sharding import PartitionSpec as P

MESH = pl.DeviceIdType.MESH
F32 = jnp.float32
BF16 = jnp.bfloat16
HEADS = 12
KVH = 4
HD = 128
PAGE = 128
TEN = 16
REP = 32
D = 1536
NEG = -1e30
SCALE = HD ** (-0.5)
FAR_FIRST = (8, 7, 9, 6, 10, 5, 11, 4, 12, 3, 13, 2, 14, 1, 15)


def replica_offsets():
    pairs = [(dx, dz) for dx in range(4) for dz in range(8) if (dx, dz) != (0, 0)]
    return sorted(pairs, key=lambda p: -(min(p[0], 4 - p[0]) + min(p[1], 8 - p[1])))


def iota(shape, dim):
    return lax.broadcasted_iota(jnp.int32, shape, dim)


def normed(rows, gain):
    inverse = lax.rsqrt(jnp.mean(rows * rows, axis=-1, keepdims=True) + 1e-05)
    return (rows * inverse * gain).astype(BF16)


def dot(a, b):
    return jnp.dot(a, b, preferred_element_type=F32)


def dot_t(a, b):
    return lax.dot_general(a, b, (((1,), (1,)), ((), ())), preferred_element_type=F32)


def per_head_rows(parts):
    kv_of = iota((16, HD), 0) // 3
    result = jnp.broadcast_to(parts[0], (16, HD))
    for k in range(1, KVH):
        result = jnp.where(kv_of == k, jnp.broadcast_to(parts[k], (16, HD)), result)
    return result


def block_queries(query):
    kv_of = iota((16, HD), 0) // 3
    return jnp.concatenate(
        [jnp.where(kv_of == k, query, 0.0) for k in range(KVH)], axis=1
    ).astype(BF16)


def own_lanes(wide):
    kv_of = iota((16, HD), 0) // 3
    result = wide[:, :HD]
    for k in range(1, KVH):
        result = jnp.where(kv_of == k, wide[:, k * HD : (k + 1) * HD], result)
    return result


def pack_terms(summed, peak, total):
    row, lane = iota((16, HD), 0), iota((16, HD), 1)
    live = row < HEADS
    spread = jnp.where(live & (lane == row), peak, 0.0) + jnp.where(
        live & (lane == row + 16), total, 0.0
    )
    stats = jnp.sum(spread, axis=0, keepdims=True)
    high = stats.astype(BF16).astype(F32)
    rest = stats - high
    middle = rest.astype(BF16).astype(F32)
    low = (rest - middle).astype(BF16).astype(F32)
    slab = jnp.where(live, summed, 0.0)
    for r, piece in ((12, high), (13, middle), (14, low)):
        slab = jnp.where(row == r, jnp.broadcast_to(piece, (16, HD)), slab)
    return slab.astype(BF16)


def unpack_terms(slab):
    row, lane = iota((16, HD), 0), iota((16, HD), 1)
    wide = slab.astype(F32)
    stats = jnp.broadcast_to(
        (wide[12:13] + wide[13:14]) + wide[14:15], (16, HD)
    )
    peak = jnp.sum(jnp.where(lane == row, stats, 0.0), axis=1, keepdims=True)
    total = jnp.sum(jnp.where(lane == row + 16, stats, 0.0), axis=1, keepdims=True)
    return wide, peak, total


def page_terms(query, keys, values, limits):
    blocks = block_queries(query)
    lane = iota((16, PAGE), 1)
    scores, usable = [], []
    for key, limit in zip(keys, limits):
        ok = lane < limit
        usable.append(ok)
        scores.append(jnp.where(ok, dot_t(blocks, key) * SCALE, NEG))
    peak = jnp.max(scores[0], axis=1, keepdims=True)
    for s in scores[1:]:
        peak = jnp.maximum(peak, jnp.max(s, axis=1, keepdims=True))
    weights = [jnp.where(ok, jnp.exp(s - peak), 0.0) for ok, s in zip(usable, scores)]
    total = sum(jnp.sum(w, axis=1, keepdims=True) for w in weights)
    wide = sum(dot(w.astype(BF16), v) for w, v in zip(weights, values))
    return own_lanes(wide), peak, total


def kernel(
    tok_ref, again_ref, mgain_ref, pt_ref, routes_ref,
    pt_s, hl_s, gs_s, gp_s, gl_s,
    wqkv_h, wo_h, router_h, wgu_h, wd_h, kv_h,
    out_ref,
    wqkv_v, wo_v, router_v, wgu_v, wd_v, kv_v,
    a_send, a_land, b_send, b_land, c_send, c_land, d_send, d_land,
    m_send, m_land, eh_send, eh_land, eg_send, eg_land,
    gh_send, gh_land, gg_send, gg_land, hh_send, hh_land, hg_send, hg_land,
    x_s, t_s, p_s, att_s, e_s, hid_s, y_s, mask_s,
    wsem, ssem, rsem,
):
    col = lax.axis_index("tensor")
    rep = lax.axis_index("replica")
    rx, rz = rep // 8, rep % 8
    ten_devs = [(k, (rep, lax.rem(col + k, TEN)), lax.rem(col + k, TEN)) for k in FAR_FIRST]
    rep_devs = [
        (lax.rem(rx + dx, 4) * 8 + lax.rem(rz + dz, 8), col) for dx, dz in replica_offsets()
    ]

    loads = [
        pltpu.make_async_copy(src, dst, wsem.at[i])
        for i, (src, dst) in enumerate(
            (
                (wqkv_h, wqkv_v), (kv_h, kv_v), (wgu_h, wgu_v),
                (wd_h, wd_v), (router_h, router_v),
            )
        )
    ]
    for load in loads:
        load.start()
    load_qkv, load_kv, load_gu, load_down, load_router = loads

    barrier = pltpu.get_barrier_semaphore()
    for dev in rep_devs:
        pl.semaphore_signal(barrier, inc=1, device_id=dev, device_id_type=MESH)
    for _, dev, _ in ten_devs:
        pl.semaphore_signal(barrier, inc=1, device_id=dev, device_id_type=MESH)

    def remote(src, dst, phase, dev):
        pltpu.make_async_remote_copy(
            src_ref=src, dst_ref=dst, send_sem=ssem.at[phase], recv_sem=rsem.at[phase],
            device_id=dev, device_id_type=MESH,
        ).start()

    def arrived(land, phase):
        pltpu.make_async_copy(land, land, rsem.at[phase]).wait()

    def gather(send, land, phase):
        for _, dev, _ in ten_devs:
            remote(send, land.at[col], phase, dev)
        pltpu.make_async_copy(send, land.at[col], rsem.at[phase]).start()

    def scatter(send, land, phase):
        for _, dev, other in ten_devs:
            remote(send.at[other], land.at[col], phase, dev)
        pltpu.make_async_copy(send.at[col], land.at[col], rsem.at[phase]).start()

    def gather_far(send, land, phase):
        for dev in rep_devs:
            remote(send, land.at[rep], phase, dev)
        pltpu.make_async_copy(send, land.at[rep], rsem.at[phase]).start()

    rows = tok_ref[...].astype(F32)
    a_send[:, :D] = rows[0:2].astype(BF16)
    a_send[:, D:] = jnp.concatenate(
        [rows[2:3, : D // 2], rows[2:3, D // 2 :]], axis=0
    ).astype(BF16)
    pl.semaphore_wait(barrier, TEN - 1 + REP - 1)
    gather(a_send, a_land, 0)

    lane, row = iota((32, 128), 1), iota((32, 128), 0)
    dest, place = lane >> 3, lane & 7
    target = jnp.where(place < 4, dest * 6 + place, -1)
    first, second = pt_ref[:, 0:1], pt_ref[:, 1:2]
    top = (
        (first == target)
        | (second == target)
        | ((place >= 4) & (place < 6) & (row == dest * 2 + place - 4))
    )
    glane, grow = iota((16, 128), 1), iota((16, 128), 0)
    bottom = ((glane & 7) == 6) & (grow == (glane >> 3))
    picks_t = jnp.concatenate(
        [
            jnp.where(top, 1.0, 0.0),
            jnp.where(bottom, 1.0, 0.0),
            jnp.zeros((80, 128), F32),
        ],
        axis=0,
    )
    picks = jnp.transpose(picks_t)[:, :48].astype(BF16)

    rlane = iota((48, 128), 1)
    routed = rlane < 0
    for k in range(6):
        routed = routed | (routes_ref[:, k : k + 1] == rlane)
    new, old = iota((48, 48), 0), iota((48, 48), 1)
    source_row = jnp.where(new < 32, (new >> 1) * 3 + (new & 1), (new - 32) * 3 + 2)
    order = jnp.where(old == source_row, 1.0, 0.0).astype(BF16)
    mask_s[...] = dot(order, jnp.where(routed, 1.0, 0.0).astype(BF16))

    base = col * 6

    def page_limits(j, limits):
        length = hl_s[j]
        one, two = pt_s[j, 0] - base, pt_s[j, 1] - base
        return tuple(
            limit + jnp.where(one == p, length, 0) + jnp.where(two == p, length - PAGE, 0)
            for p, limit in enumerate(limits)
        )

    limits = lax.fori_loop(0, 32, page_limits, (jnp.int32(0),) * 4)

    for _, dev, other in ten_devs:
        @pl.when(other < 12)
        def _():
            at = pl.multiple_of(other * 128, 128)
            remote(
                wo_h.at[:, pl.ds(at, 128)],
                wo_v.at[pl.ds(pl.multiple_of(col * 96, 96), 96), :],
                13, dev,
            )

    @pl.when(col < 12)
    def _():
        at = pl.multiple_of(col * 128, 128)
        pltpu.make_async_copy(
            wo_h.at[:, pl.ds(at, 128)],
            wo_v.at[pl.ds(pl.multiple_of(col * 96, 96), 96), :],
            rsem.at[13],
        ).start()

    arrived(a_land, 0)
    for c in range(TEN):
        slab = a_land[c].astype(F32)
        t_s[2 * c : 2 * c + 2, :] = slab[:, :D]
        t_s[32 + c : 33 + c, : D // 2] = slab[0:1, D:]
        t_s[32 + c : 33 + c, D // 2 :] = slab[1:2, D:]
    load_qkv.wait()
    projected = dot(normed(t_s[...], again_ref[...]), wqkv_v[...]).astype(BF16)
    chosen = dot(picks, projected)
    shift = lax.rem(col * 5, 4) * 32
    chosen = pltpu.roll(
        jnp.concatenate([chosen, jnp.zeros((128, 96), F32)], axis=1), shift, 1
    )
    for c in range(TEN):
        b_send[c] = chosen[8 * c : 8 * c + 8].astype(BF16)
    scatter(b_send, b_land, 1)

    arrived(b_land, 1)
    blocks = [None] * 20
    for c in range(TEN):
        slab = b_land[c].astype(F32)
        at = (5 * c) // 4
        for n, piece in ((at, slab[:, :128]), (at + 1, slab[:, 128:])):
            blocks[n] = piece if blocks[n] is None else blocks[n] + piece
    for n in range(20):
        p_s[8 * n : 8 * n + 8, :] = blocks[n]

    def heads_of(r):
        return p_s[pl.ds(r, 16, stride=8), :]

    def fresh_of(r, start):
        return per_head_rows([p_s[8 * (start + k) + r : 8 * (start + k) + r + 1, :] for k in range(KVH)])

    row16 = iota((16, HD), 0)
    slab = heads_of(6)
    for r, number in ((12, gs_s[0]), (13, gl_s[0]), (14, gp_s[0, 0]), (15, gp_s[0, 1])):
        slab = jnp.where(row16 == r, jnp.full((16, HD), number, jnp.int32).astype(F32), slab)
    c_send[...] = slab.astype(BF16)
    gather_far(c_send, c_land, 2)

    load_kv.wait()
    for p in range(4):
        summed, peak, total = page_terms(heads_of(p), [kv_v[p, 0]], [kv_v[p, 1]], [limits[p]])
        m_send[p] = pack_terms(summed, peak, total)
    gather(m_send, m_land, 4)

    arrived(c_land, 2)
    mine = jnp.full((16, HD), rep, jnp.int32).astype(F32)
    served = jnp.zeros((16, HD), F32)
    for r in range(REP):
        slab = c_land[r].astype(F32)
        served = jnp.where(jnp.broadcast_to(slab[12:13], (16, HD)) == mine, slab, served)
    length = served[13:14]
    page_a, page_b = served[14:15], served[15:16]
    far_limits = [
        jnp.broadcast_to(
            jnp.where(page_a == p, length, jnp.where(page_b == p, length - PAGE, 0.0)), (16, HD)
        ).astype(jnp.int32)
        for p in (4.0, 5.0)
    ]
    summed, peak, total = page_terms(
        served, [kv_v[4, 0], kv_v[5, 0]], [kv_v[4, 1], kv_v[5, 1]], far_limits
    )
    d_send[...] = pack_terms(summed, peak, total)
    gather_far(d_send, d_land, 3)

    def finish(r, terms):
        query = heads_of(r)
        own = jnp.sum(query * fresh_of(r, 12), axis=1, keepdims=True) * SCALE
        highest = own
        for _, peak, _ in terms:
            highest = jnp.maximum(highest, peak)
        newest = jnp.exp(own - highest)
        top_sum = newest * fresh_of(r, 16)
        bottom_sum = newest
        for summed, peak, total in terms:
            factor = jnp.exp(peak - highest)
            top_sum = top_sum + factor * summed
            bottom_sum = bottom_sum + factor * total
        return top_sum / bottom_sum

    arrived(m_land, 4)
    for s in range(2):
        terms = []
        for k in range(2):
            page = pt_s[2 * col + s, k]
            terms.append(unpack_terms(m_land[page // 6, page % 6]))
        att_s[16 * s : 16 * s + 16, :] = finish(4 + s, terms)
    eh_send[...] = jnp.concatenate(
        [att_s[pl.ds(h, 2, stride=16), :] for h in range(HEADS)], axis=1
    ).astype(BF16)
    gather(eh_send, eh_land, 5)

    arrived(d_land, 3)
    att_s[32:48, :] = finish(6, [unpack_terms(d_land[gs_s[0]])])
    eg_send[...] = jnp.concatenate(
        [att_s[pl.ds(32 + h, 2, stride=6), :] for h in range(HEADS // 2)], axis=1
    ).astype(BF16)
    gather(eg_send, eg_land, 6)

    mine_at = pl.multiple_of(jnp.where(col < 12, col, 0) * 128, 128)

    def to_columns(send, land, phase):
        for _, dev, _ in ten_devs:
            remote(send, land.at[col], phase, dev)
        pltpu.make_async_copy(send, land.at[col], rsem.at[phase]).start()

    def stage(land, start, guests):
        for c in range(TEN):
            slab = land[c].astype(F32)
            if guests:
                e_s[start + c : start + c + 1, : D // 2] = slab[0:1]
                e_s[start + c : start + c + 1, D // 2 :] = slab[1:2]
            else:
                e_s[start + 2 * c : start + 2 * c + 2, :] = slab

    arrived(eh_land, 5)

    @pl.when(col < 12)
    def _():
        arrived(wo_v, 13)
        stage(eh_land, 0, False)
        part = dot(e_s[0:32, :].astype(BF16), wo_v[...])
        gh_send[...] = (t_s[0:32, pl.ds(mine_at, 128)] + part).astype(BF16)
        to_columns(gh_send, gh_land, 7)

    arrived(eg_land, 6)

    @pl.when(col < 12)
    def _():
        stage(eg_land, 32, True)
        part = dot(e_s[32:48, :].astype(BF16), wo_v[...])
        gg_send[...] = (t_s[32:48, pl.ds(mine_at, 128)] + part).astype(BF16)
        to_columns(gg_send, gg_land, 8)

    def experts(land, start, count):
        hidden = jnp.concatenate([land[n] for n in range(12)], axis=1).astype(F32)
        hid_s[start : start + count, :] = hidden
        rows = normed(hidden, mgain_ref[...])
        logits = dot(rows, router_v[...])
        mask = mask_s[start : start + count, 0:8] > 0.5
        highest = jnp.max(jnp.where(mask, logits, NEG), axis=1, keepdims=True)
        powers = jnp.where(mask, jnp.exp(logits - highest), 0.0)
        here = jnp.where(iota((count, 8), 1) == col // 2, powers, 0.0)
        weight = jnp.sum(here, axis=1, keepdims=True) / jnp.sum(powers, axis=1, keepdims=True)
        both = dot(rows, wgu_v[...])
        gate, upper = both[:, :256], both[:, 256:]
        activated = (gate / (1.0 + jnp.exp(-gate)) * upper * weight).astype(BF16)
        y_s[start : start + count, :] = dot(activated, wd_v[...])

    arrived(gh_land, 7)
    load_router.wait()
    load_gu.wait()
    load_down.wait()
    experts(gh_land, 0, 32)
    for c in range(TEN):
        hh_send[c] = y_s[2 * c : 2 * c + 2, :].astype(BF16)
    scatter(hh_send, hh_land, 9)

    arrived(gg_land, 8)
    experts(gg_land, 32, 16)
    for c in range(TEN):
        hg_send[c] = jnp.concatenate(
            [y_s[32 + c : 33 + c, : D // 2], y_s[32 + c : 33 + c, D // 2 :]], axis=0
        ).astype(BF16)
    scatter(hg_send, hg_land, 10)

    def own_rows(start, at):
        tile = hid_s[pl.ds(pl.multiple_of(start + at // 8 * 8, 8), 8), :]
        return pltpu.roll(tile, lax.rem(8 - at % 8, 8), 0)

    arrived(hh_land, 9)
    total = hh_land[0].astype(F32)
    for c in range(1, TEN):
        total = total + hh_land[c].astype(F32)
    home = own_rows(0, 2 * col)[0:2] + total
    arrived(hg_land, 10)
    total = hg_land[0].astype(F32)
    for c in range(1, TEN):
        total = total + hg_land[c].astype(F32)
    guest = own_rows(32, col)[0:1] + jnp.concatenate([total[0:1], total[1:2]], axis=1)
    out_ref[...] = jnp.concatenate([home, guest], axis=0).astype(BF16)

    def left(land, count, phase):
        pltpu.make_async_copy(land.at[pl.ds(0, count)], land.at[pl.ds(0, count)], ssem.at[phase]).wait()

    for land, count, phase in (
        (a_land, 15, 0), (b_land, 15, 1), (c_land, 31, 2), (d_land, 31, 3), (m_land, 15, 4),
        (eh_land, 15, 5), (eg_land, 15, 6), (hh_land, 15, 9), (hg_land, 15, 10),
    ):
        left(land, count, phase)

    @pl.when(col < 12)
    def _():
        for src, dst, phase in ((gh_send, gh_land.at[0], 7), (gg_send, gg_land.at[0], 8)):
            for _ in range(15):
                pltpu.make_async_copy(src, dst, ssem.at[phase]).wait()
        pltpu.make_async_copy(wo_v.at[pl.ds(0, 96 * 11), :], wo_v.at[pl.ds(0, 96 * 11), :], ssem.at[13]).wait()

    @pl.when(col >= 12)
    def _():
        pltpu.make_async_copy(wo_v.at[pl.ds(0, 96 * 12), :], wo_v.at[pl.ds(0, 96 * 12), :], ssem.at[13]).wait()


def shards(
    tokens, attn_gain, qkv_weight, out_weight, moe_gain, router, expert_gate_up,
    expert_down, kv_cache, page_table, home_len, guest_source, guest_pages, guest_len, routes,
):
    vmem = pl.BlockSpec(memory_space=pltpu.VMEM)
    smem = pl.BlockSpec(memory_space=pltpu.SMEM)
    hbm = pl.BlockSpec(memory_space=pl.ANY)
    V = pltpu.VMEM
    return pl.pallas_call(
        kernel,
        out_shape=jax.ShapeDtypeStruct((3, D), BF16),
        in_specs=[vmem] * 5 + [smem] * 5 + [hbm] * 6,
        out_specs=vmem,
        scratch_shapes=[
            V((D, 160), BF16), V((D, 128), BF16), V((D, 8), BF16), V((D, 512), BF16),
            V((256, D), BF16), V((6, 2, 128, 512), BF16),
            V((2, 2304), BF16), V((TEN, 2, 2304), BF16),
            V((TEN, 8, 256), BF16), V((TEN, 8, 256), BF16),
            V((16, 128), BF16), V((REP, 16, 128), BF16),
            V((16, 128), BF16), V((REP, 16, 128), BF16),
            V((4, 16, 128), BF16), V((TEN, 4, 16, 128), BF16),
            V((2, D), BF16), V((TEN, 2, D), BF16),
            V((2, D // 2), BF16), V((TEN, 2, D // 2), BF16),
            V((32, 128), BF16), V((12, 32, 128), BF16),
            V((16, 128), BF16), V((12, 16, 128), BF16),
            V((TEN, 2, D), BF16), V((TEN, 2, D), BF16),
            V((TEN, 2, D // 2), BF16), V((TEN, 2, D // 2), BF16),
            V((8, 128), F32), V((48, D), F32), V((160, 128), F32), V((48, 128), F32),
            V((48, D), F32), V((48, D), F32), V((48, D), F32), V((48, 128), F32),
            pltpu.SemaphoreType.DMA((5,)),
            pltpu.SemaphoreType.DMA((14,)),
            pltpu.SemaphoreType.DMA((14,)),
        ],
        compiler_params=pltpu.CompilerParams(
            collective_id=0, has_side_effects=True, vmem_limit_bytes=48 << 20
        ),
    )(
        tokens, attn_gain.reshape(1, D), moe_gain.reshape(1, D), page_table, routes,
        page_table, home_len, guest_source, guest_pages, guest_len,
        qkv_weight, out_weight, router, expert_gate_up.reshape(D, 512), expert_down, kv_cache,
    )


def solution(mesh):
    placed = (
        P(("replica", "tensor"), None),
        P(),
        P(None, "tensor"),
        P("tensor", None),
        P(),
        P(),
        P(None, None, "tensor"),
        P("tensor", None),
        P(("replica", "tensor"), None, None, None),
        P("replica", None),
        P("replica"),
        P(("replica", "tensor")),
        P(("replica", "tensor"), None),
        P(("replica", "tensor")),
        P("replica", None),
    )
    return jax.shard_map(
        shards,
        mesh=mesh,
        in_specs=placed,
        out_specs=P(("replica", "tensor"), None),
        check_vma=False,
    )
```
